512 devices in a mesh: gx: 16 (over x, z_hi, core), gy: 32 (over z_lo, y).
Axes of the slice: x: 4, y: 4, z: 16 (z_hi: 2, z_lo: 8; z = z_hi * 8 + z_lo), core: 2. Of those that a mesh axis runs over, the one named last changes fastest.
Arguments:
- fine_multipoles: bfloat16 [32, 32, 32, 2, 256], P('gx', 'gy'), may hold values from -6 to 6
- m2m_ops: bfloat16 [2, 2, 2, 256, 256], replicated, may hold values from -0.125 to 0.125
- m2l_ops: bfloat16 [512, 256, 256], P('gy'), may hold values from -0.015625 to 0.015625
- offsets: int32 [512, 3], P('gy'), may hold values from -7 to 7, as said below
Outputs:
- local_expansions: float32 [16, 256, 2, 256], P('gx', 'gy')
The draws below stay inside these ranges and needn't reach their ends.
Inputs may be any that keep to these rules, and one draw needn't show every extreme that they name: Rows are distinct offsets; the first component lies in -3 to 3; in each row the largest magnitude of the three components is 2 or more.
All inputs are finite; a program needn't handle non-finite values.
Results may differ from the reference program's by a relative error of at most 0.0029.
Values may be sent and summed in bfloat16 or wider, within the bound.
A program may use at most 64 MiB of HBM per device.

```python
import jax
import jax.numpy as jnp
import numpy as np
from jax import lax

C = 256
RHS = 2
ZB = 32
FX = 32
FY = 32
CX = 16
CY = 16
CZ = 16
OFFS = 512


def draw_offsets(key, part):
    lattice = np.array([(a, b, c) for a in range(-3, 4) for b in range(-7, 8) for c in range(-7, 8) if max(abs(a), abs(b), abs(c)) >= 2 and (a, b, c) != (3, 7, 7) and ((a, b, c) != (-3, -7, -7))], dtype=np.int32)
    shuffle_key, order_key = jax.random.split(jax.random.fold_in(key, 11))
    remaining = jax.random.permutation(shuffle_key, jnp.asarray(lattice), axis=0)
    extremes = jnp.array([[3, 7, 7], [-3, -7, -7]], jnp.int32)
    chosen = jnp.concatenate([extremes, remaining[:OFFS - 2]], axis=0)
    return jax.random.permutation(order_key, chosen, axis=0)


def shard_levels(key, extent, cuts, smallest, high):
    def one(dim, parts):
        draws = jax.random.uniform(jax.random.fold_in(jax.random.fold_in(key, 6), dim), (parts,), jnp.float32, smallest / len(cuts), high / len(cuts))
        return jnp.repeat(jnp.exp(draws), extent[dim] // parts).reshape((-1,) + (1,) * (len(extent) - dim - 1))

    loudness = one(*cuts[0])
    for cut in cuts[1:]:
        loudness = loudness * one(*cut)
    return loudness


def noise(own_key, shape, deviation, reach, cuts=(), held_as=jnp.bfloat16):
    drawn = jax.random.normal(own_key, shape, jnp.float32) * deviation
    if len(cuts) > 0:
        drawn = shard_levels(own_key, shape, cuts, -0.22, 0.18) * drawn
    return jnp.clip(drawn, min=-reach, max=reach).astype(held_as)


def setup_inputs(seed: int = 0) -> dict:
    arg_keys = jax.random.split(jax.random.key(seed), 5)
    return {
        "fine_multipoles": noise(arg_keys[0], (FX, FY, ZB, RHS, C), 1.0, 6.0, ((0, 16), (1, 32))),
        "m2m_ops": noise(arg_keys[1], (2, 2, 2, C, C), (8 * C) ** -0.5, 0.125),
        "m2l_ops": noise(arg_keys[2], (OFFS, C, C), (OFFS * C) ** -0.5, 0.015625, ((0, 32),)),
        "offsets": draw_offsets(jax.random.fold_in(arg_keys[4], 71), 0),
    }


def reference(fine_multipoles, m2m_ops, m2l_ops, offsets):
    blocks = fine_multipoles.astype(jnp.float32).reshape(CX, 2, CY, 2, CZ, 2, RHS, C)
    coarse = jnp.einsum("xaybzcri,abcio->xyzro", blocks, m2m_ops.astype(jnp.float32)).astype(jnp.bfloat16)

    def accumulate(summed, op_index):
        shift_row = offsets[op_index]
        source = jnp.roll(coarse, (-shift_row[0], -shift_row[1], -shift_row[2]), axis=(0, 1, 2))
        term_rows = jnp.dot(source.reshape(CX * CY * CZ * RHS, C).astype(jnp.float32), m2l_ops[op_index].astype(jnp.float32))
        return summed + term_rows, None

    summed, unused = lax.scan(accumulate, jnp.zeros((CX * CY * CZ * RHS, C), jnp.float32), jnp.arange(OFFS))
    return summed.reshape(CX, CY * CZ, RHS, C)
```

```python
import functools

import jax
import jax.numpy as jnp
from jax import lax
from jax.experimental import pallas as pl
from jax.experimental.pallas import tpu as pltpu
from jax.sharding import PartitionSpec as P

MESH = pl.DeviceIdType.MESH
VMEM = pl.BlockSpec(memory_space=pltpu.VMEM)
SMEM = pl.BlockSpec(memory_space=pltpu.SMEM)


def place():
    gx, gy = lax.axis_index("gx"), lax.axis_index("gy")
    return gx // 4, gx // 2 % 2, gx % 2, gy // 4, gy % 4


def device(x, zh, core, zl, y):
    return (x * 4 + zh * 2 + core, zl * 4 + y)


def greet(peers):
    barrier = pltpu.get_barrier_semaphore()
    for peer in peers:
        pl.semaphore_signal(barrier, inc=1, device_id=peer, device_id_type=MESH)
    pl.semaphore_wait(barrier, len(peers))


def first_shared(zh_block, zh, sender_core):
    return jnp.where(zh_block < zh, 1, jnp.where(zh_block > zh, 0, 1 - sender_core))


def gather_kernel(mine, held, other, local_sem, x_send, x_recv, y_send, y_recv, r_send, r_recv, l_send, l_recv, c_send, c_recv):
    x, zh, core, zl, y = place()
    zp = zh * 8 + zl
    after = (zp + 1) % 16
    before = (zp + 15) % 16
    x_next = device((x + 1) % 4, zh, core, zl, y)
    x_last = device((x + 3) % 4, zh, core, zl, y)
    y_peers = [device(x, zh, core, zl, (y + d) % 4) for d in (1, 2, 3)]
    z_next = device(x, after // 8, core, after % 8, y)
    z_last = device(x, before // 8, core, before % 8, y)
    partner = device(x, zh, 1 - core, zl, y)

    def remote(src, dst, send, recv, target):
        return pltpu.make_async_remote_copy(
            src_ref=src, dst_ref=dst, send_sem=send, recv_sem=recv, device_id=target, device_id_type=MESH
        )

    own = pltpu.make_async_copy(mine, held.at[zp, 1, y], local_sem)
    own.start()
    greet([x_next, x_last, *y_peers, z_next, z_last, partner])
    along_x = [
        remote(mine, held.at[zp, 0, y], x_send.at[0], x_recv.at[0], x_next),
        remote(mine, held.at[zp, 2, y], x_send.at[1], x_recv.at[1], x_last),
    ]
    for copy in along_x:
        copy.start()
    own.wait()
    for copy in along_x:
        copy.wait()
    along_y = [
        remote(held.at[zp, :, y], held.at[zp, :, y], y_send.at[d], y_recv.at[d], y_peers[d]) for d in range(3)
    ]
    for copy in along_y:
        copy.start()
    for copy in along_y:
        copy.wait()

    def right(step, slot):
        block = held.at[(zp + 16 - step) % 16, slot]
        return remote(block, block, r_send.at[step, slot], r_recv.at[step, slot], z_next)

    def left(step, slot):
        block = held.at[(zp + step) % 16, slot]
        return remote(block, block, l_send.at[step, slot], l_recv.at[step, slot], z_last)

    def share(position):
        start = first_shared(position // 8, zh, core)
        return remote(held.at[position, pl.ds(start, 2)], other.at[position], c_send.at[position], c_recv.at[position], partner)

    for slot in range(3):
        right(0, slot).start()
        left(0, slot).start()
    share(zp).start()

    def advance(step, carry):
        for slot in range(3):
            right(step - 1, slot).wait_recv()
            right(step, slot).start()
            left(step - 1, slot).wait_recv()

            @pl.when(step < 7)
            def _():
                left(step, slot).start()

        share((zp + 16 - step) % 16).start()
        share((zp + step) % 16).start()
        return carry

    lax.fori_loop(1, 8, advance, 0)
    for slot in range(3):
        right(7, slot).wait_recv()
    share((zp + 8) % 16).start()

    def drain(step, carry):
        for slot in range(3):
            right(step, slot).wait_send()

            @pl.when(step < 7)
            def _():
                left(step, slot).wait_send()

        share(step).wait()
        share(step + 8).wait()
        return carry

    lax.fori_loop(0, 8, drain, 0)


def gather_planes(mine):
    dma = pltpu.SemaphoreType.DMA
    return pl.pallas_call(
        gather_kernel,
        out_shape=[
            jax.ShapeDtypeStruct((16, 3, 4, 16, 256), jnp.bfloat16),
            jax.ShapeDtypeStruct((16, 2, 4, 16, 256), jnp.bfloat16),
        ],
        in_specs=[VMEM],
        out_specs=[VMEM, VMEM],
        scratch_shapes=[
            dma,
            dma((2,)), dma((2,)),
            dma((3,)), dma((3,)),
            dma((8, 3)), dma((8, 3)),
            dma((7, 3)), dma((7, 3)),
            dma((16,)), dma((16,)),
        ],
        compiler_params=pltpu.CompilerParams(collective_id=0, has_side_effects=True),
        name="gather_planes",
    )(mine)


def translate_kernel(spot, offsets, held, other, ops, out, planes, total):
    zh, core = spot[0], spot[1]
    for shift in range(-3, 4):
        reach = shift + zh * 2 + core + 4
        slot = reach // 4
        zh_from = reach % 4 // 2
        if shift % 2:
            slot = slot - first_shared(zh_from, zh, 1 - core)
        source = other if shift % 2 else held
        for zl in range(8):
            rows = source[zh_from * 8 + zl, slot].astype(jnp.float32)
            for half in range(2):
                line = rows[half * 32 : half * 32 + 32]
                for part in range(2):
                    piece = line[:, part * 128 : part * 128 + 128]
                    planes[part, shift + 3, zl * 2 + half, 0:32] = piece
                    planes[part, shift + 3, zl * 2 + half, 32:64] = piece
    total[...] = jnp.zeros_like(total)

    def one(entry, carry):
        dx, dy, dz = offsets[entry, 0] + 3, offsets[entry, 1], offsets[entry, 2]
        start = 2 * ((dz + 16) & 15)
        halves = [
            jnp.concatenate([planes[part, dx, (line + dy + 16) & 15, pl.ds(start, 32), :] for line in range(16)], axis=0)
            for part in range(2)
        ]
        rolled = jnp.concatenate(halves, axis=1).astype(jnp.bfloat16)
        total[...] += jnp.dot(rolled, ops[entry], preferred_element_type=jnp.float32)
        return carry

    lax.fori_loop(0, 16, one, 0)
    out[...] = total[...].astype(jnp.bfloat16)


def translate(spot, offsets, held, other, ops):
    return pl.pallas_call(
        translate_kernel,
        out_shape=jax.ShapeDtypeStruct((512, 256), jnp.bfloat16),
        in_specs=[SMEM, SMEM, VMEM, VMEM, VMEM],
        out_specs=VMEM,
        scratch_shapes=[pltpu.VMEM((2, 7, 16, 64, 128), jnp.float32), pltpu.VMEM((512, 256), jnp.float32)],
        name="translate",
    )(spot, offsets, held, other, ops)


def scatter_kernel(part, out, from_y, summed, rounded, from_z, y_send, y_recv, z_send, z_recv):
    x, zh, core, zl, y = place()
    y_of = [(y + d) % 4 for d in (1, 2, 3)]
    z_of = [(zl + d) % 8 for d in range(1, 8)]
    y_peers = [device(x, zh, core, zl, to) for to in y_of]
    z_peers = [device(x, zh, core, to, y) for to in z_of]
    greet(y_peers + z_peers)
    along_y = [
        pltpu.make_async_remote_copy(
            src_ref=part.at[:, y_of[d]], dst_ref=from_y.at[d], send_sem=y_send.at[d], recv_sem=y_recv.at[d],
            device_id=y_peers[d], device_id_type=MESH,
        )
        for d in range(3)
    ]
    for copy in along_y:
        copy.start()
    for copy in along_y:
        copy.wait()
    row = part[:, y].astype(jnp.float32)
    for d in range(3):
        row = row + from_y[d].astype(jnp.float32)
    summed[...] = row
    rounded[...] = row.astype(jnp.bfloat16)
    along_z = [
        pltpu.make_async_remote_copy(
            src_ref=rounded.at[z_of[d]], dst_ref=from_z.at[d], send_sem=z_send.at[d], recv_sem=z_recv.at[d],
            device_id=z_peers[d], device_id_type=MESH,
        )
        for d in range(7)
    ]
    for copy in along_z:
        copy.start()
    for copy in along_z:
        copy.wait()
    result = summed[zl]
    for d in range(7):
        result = result + from_z[d].astype(jnp.float32)
    out[...] = result


def scatter_sums(part):
    dma = pltpu.SemaphoreType.DMA
    return pl.pallas_call(
        scatter_kernel,
        out_shape=jax.ShapeDtypeStruct((16, 256), jnp.float32),
        in_specs=[VMEM],
        out_specs=VMEM,
        scratch_shapes=[
            pltpu.VMEM((3, 8, 16, 256), jnp.bfloat16),
            pltpu.VMEM((8, 16, 256), jnp.float32),
            pltpu.VMEM((8, 16, 256), jnp.bfloat16),
            pltpu.VMEM((7, 16, 256), jnp.bfloat16),
            dma((3,)), dma((3,)), dma((7,)), dma((7,)),
        ],
        compiler_params=pltpu.CompilerParams(collective_id=1, has_side_effects=True),
        name="scatter_sums",
    )(part)


def on_device(fine_multipoles, m2m_ops, m2l_ops, offsets):
    parity = lax.axis_index("gy") % 2
    selected = lax.dynamic_index_in_dim(m2m_ops, parity, 1, keepdims=False)
    children = fine_multipoles[:, 0].reshape(2, 16, 2, 2, 256)
    partial = jnp.einsum("azcri,acio->zro", children, selected, preferred_element_type=jnp.float32)
    kept = lax.dynamic_slice_in_dim(partial, parity * 8, 8, 0)
    sent = lax.dynamic_slice_in_dim(partial, (1 - parity) * 8, 8, 0)
    arrived = lax.ppermute(sent, "gy", [(i, i ^ 1) for i in range(32)])
    mine = (kept + arrived).astype(jnp.bfloat16).reshape(16, 256)
    held, other = gather_planes(mine)
    gx = lax.axis_index("gx")
    spot = jnp.stack([gx // 2 % 2, gx % 2]).astype(jnp.int32)
    part = translate(spot, offsets, held.reshape(16, 3, 64, 256), other.reshape(16, 2, 64, 256), m2l_ops)
    result = scatter_sums(part.reshape(8, 4, 16, 256))
    return result.reshape(1, 8, 2, 256)


def solution(mesh):
    return jax.shard_map(
        on_device,
        mesh=mesh,
        in_specs=(P("gx", "gy", None, None, None), P(), P("gy", None, None), P("gy", None)),
        out_specs=P("gx", "gy", None, None),
        check_vma=False,
    )
```

```python
import functools

import jax
import jax.numpy as jnp
from jax import lax
from jax.experimental import pallas as pl
from jax.experimental.pallas import tpu as pltpu
from jax.sharding import PartitionSpec as P

MESH = pl.DeviceIdType.MESH
VMEM = pl.BlockSpec(memory_space=pltpu.VMEM)
SMEM = pl.BlockSpec(memory_space=pltpu.SMEM)


def place():
    gx, gy = lax.axis_index("gx"), lax.axis_index("gy")
    return gx // 4, gx // 2 % 2, gx % 2, gy // 4, gy % 4


def device(x, zh, core, zl, y):
    return (x * 4 + zh * 2 + core, zl * 4 + y)


def greet(peers):
    barrier = pltpu.get_barrier_semaphore()
    for peer in peers:
        pl.semaphore_signal(barrier, inc=1, device_id=peer, device_id_type=MESH)
    pl.semaphore_wait(barrier, len(peers))


def source_offset(turn):
    return jnp.where(turn % 2 == 1, (turn + 1) // 2, (16 - turn // 2) % 16)


LAG = 4


def gather_kernel(mine, held, other, local_sem, z_send, z_recv, y_send, y_recv, x_send, x_recv, c_send, c_recv):
    x, zh, core, zl, y = place()
    zp = zh * 8 + zl
    x_peers = [device((x + d) % 4, zh, core, zl, y) for d in (1, 3)]
    y_peers = [device(x, zh, core, zl, (y + d) % 4) for d in (1, 2, 3)]
    partner = device(x, zh, 1 - core, zl, y)

    def z_peer(offset):
        position = (zp + offset) % 16
        return device(x, position // 8, core, position % 8, y)

    def remote(src, dst, send, recv, target):
        return pltpu.make_async_remote_copy(
            src_ref=src, dst_ref=dst, send_sem=send, recv_sem=recv, device_id=target, device_id_type=MESH
        )

    def along_z(offset):
        to = (zp + offset) % 16
        return remote(mine, held.at[1 + core + zh - to // 8, zl, y], z_send.at[offset], z_recv.at[offset], z_peer(offset))

    def spot_of(turn):
        position = (zp + 16 - source_offset(turn)) % 16
        return position, 1 + core + position // 8 - zh, position % 8

    def along_y(turn, d):
        position, plane, row = spot_of(turn)
        piece = held.at[plane, row, y]
        return remote(piece, piece, y_send.at[position, d], y_recv.at[position, d], y_peers[d])

    def along_x(turn):
        position, plane, row = spot_of(turn)
        to = (x + jnp.where(plane >= 2, 1, 3)) % 4
        return remote(
            held.at[plane, row], held.at[(plane + 2) % 4, row], x_send.at[position], x_recv.at[position],
            device(to, zh, core, zl, y),
        )

    def across(turn, far):
        position, plane, row = spot_of(turn)
        plane = (plane + 2 * far) % 4
        return remote(held.at[plane, row], other.at[plane, row], c_send.at[position, far], c_recv.at[position, far], partner)

    own = pltpu.make_async_copy(mine, held.at[1 + core, zl, y], local_sem)
    own.start()
    greet([z_peer(d) for d in range(1, 16)] + y_peers + x_peers + [partner])

    def send_z(turn, carry):
        along_z((16 - source_offset(turn)) % 16).start()
        return carry

    lax.fori_loop(1, 16, send_z, 0)
    own.wait()

    def turns(turn, carry):
        @pl.when(turn < 16)
        def _():
            @pl.when(turn > 0)
            def _():
                along_z(source_offset(turn)).wait_recv()

            for d in range(3):
                along_y(turn, d).start()

        @pl.when((turn >= LAG) & (turn < 16 + LAG))
        def _():
            for d in range(3):
                along_y(turn - LAG, d).wait_recv()
            along_x(turn - LAG).start()
            across(turn - LAG, 0).start()

        @pl.when(turn >= 2 * LAG)
        def _():
            along_x(turn - 2 * LAG).wait_recv()
            across(turn - 2 * LAG, 1).start()

        return carry

    lax.fori_loop(0, 16 + 2 * LAG, turns, 0)

    def drain(turn, carry):
        @pl.when(turn > 0)
        def _():
            along_z(turn).wait_send()

        for d in range(3):
            along_y(turn, d).wait_send()
        along_x(turn).wait_send()
        across(turn, 0).wait()
        across(turn, 1).wait()
        return carry

    lax.fori_loop(0, 16, drain, 0)


def gather_planes(mine):
    dma = pltpu.SemaphoreType.DMA
    planes = jax.ShapeDtypeStruct((4, 8, 4, 16, 256), jnp.bfloat16)
    return pl.pallas_call(
        gather_kernel,
        out_shape=[planes, planes],
        in_specs=[VMEM],
        out_specs=[VMEM, VMEM],
        scratch_shapes=[
            dma,
            dma((16,)), dma((16,)),
            dma((16, 3)), dma((16, 3)),
            dma((16,)), dma((16,)),
            dma((16, 2)), dma((16, 2)),
        ],
        compiler_params=pltpu.CompilerParams(collective_id=0, has_side_effects=True),
        name="gather_planes",
    )(mine)


def translate_kernel(spot, offsets, held, other, ops, out, planes, total):
    for shift in range(-3, 4):
        for line in range(16):
            rows = pl.ds(line * 32, 32)
            if shift % 2:
                wide = other[(shift + 3) // 2, rows].astype(jnp.float32)
            else:
                wide = held[(shift + 2) // 2 + spot[0], rows].astype(jnp.float32)
            for part in range(2):
                piece = wide[:, part * 128 : part * 128 + 128]
                planes[part, shift + 3, line, 0:32] = piece
                planes[part, shift + 3, line, 32:64] = piece
    total[...] = jnp.zeros_like(total)

    def one(entry, carry):
        dx, dy, dz = offsets[entry, 0] + 3, offsets[entry, 1], offsets[entry, 2]
        start = 2 * ((dz + 16) & 15)
        halves = [
            jnp.concatenate([planes[part, dx, (line + dy + 16) & 15, pl.ds(start, 32), :] for line in range(16)], axis=0)
            for part in range(2)
        ]
        rolled = jnp.concatenate(halves, axis=1).astype(jnp.bfloat16)
        total[...] += jnp.dot(rolled, ops[entry], preferred_element_type=jnp.float32)
        return carry

    lax.fori_loop(0, 16, one, 0)
    out[...] = total[...].astype(jnp.bfloat16)


def translate(spot, offsets, held, other, ops):
    return pl.pallas_call(
        translate_kernel,
        out_shape=jax.ShapeDtypeStruct((512, 256), jnp.bfloat16),
        in_specs=[SMEM, SMEM, VMEM, VMEM, VMEM],
        out_specs=VMEM,
        scratch_shapes=[pltpu.VMEM((2, 7, 16, 64, 128), jnp.float32), pltpu.VMEM((512, 256), jnp.float32)],
        name="translate",
    )(spot, offsets, held, other, ops)


def scatter_kernel(part, out, from_y, summed, rounded, from_z, y_send, y_recv, z_send, z_recv):
    x, zh, core, zl, y = place()
    y_of = [(y + d) % 4 for d in (1, 2, 3)]
    z_of = [(zl + d) % 8 for d in range(1, 8)]
    y_peers = [device(x, zh, core, zl, to) for to in y_of]
    z_peers = [device(x, zh, core, to, y) for to in z_of]
    greet(y_peers + z_peers)
    along_y = [
        pltpu.make_async_remote_copy(
            src_ref=part.at[:, y_of[d]], dst_ref=from_y.at[d], send_sem=y_send.at[d], recv_sem=y_recv.at[d],
            device_id=y_peers[d], device_id_type=MESH,
        )
        for d in range(3)
    ]
    for copy in along_y:
        copy.start()
    for copy in along_y:
        copy.wait()
    row = part[:, y].astype(jnp.float32)
    for d in range(3):
        row = row + from_y[d].astype(jnp.float32)
    summed[...] = row
    rounded[...] = row.astype(jnp.bfloat16)
    along_z = [
        pltpu.make_async_remote_copy(
            src_ref=rounded.at[z_of[d]], dst_ref=from_z.at[d], send_sem=z_send.at[d], recv_sem=z_recv.at[d],
            device_id=z_peers[d], device_id_type=MESH,
        )
        for d in range(7)
    ]
    for copy in along_z:
        copy.start()
    for copy in along_z:
        copy.wait()
    result = summed[zl]
    for d in range(7):
        result = result + from_z[d].astype(jnp.float32)
    out[...] = result


def scatter_sums(part):
    dma = pltpu.SemaphoreType.DMA
    return pl.pallas_call(
        scatter_kernel,
        out_shape=jax.ShapeDtypeStruct((16, 256), jnp.float32),
        in_specs=[VMEM],
        out_specs=VMEM,
        scratch_shapes=[
            pltpu.VMEM((3, 8, 16, 256), jnp.bfloat16),
            pltpu.VMEM((8, 16, 256), jnp.float32),
            pltpu.VMEM((8, 16, 256), jnp.bfloat16),
            pltpu.VMEM((7, 16, 256), jnp.bfloat16),
            dma((3,)), dma((3,)), dma((7,)), dma((7,)),
        ],
        compiler_params=pltpu.CompilerParams(collective_id=1, has_side_effects=True),
        name="scatter_sums",
    )(part)


def on_device(fine_multipoles, m2m_ops, m2l_ops, offsets):
    parity = lax.axis_index("gy") % 2
    selected = lax.dynamic_index_in_dim(m2m_ops, parity, 1, keepdims=False)
    children = fine_multipoles[:, 0].reshape(2, 16, 2, 2, 256)
    partial = jnp.einsum("azcri,acio->zro", children, selected, preferred_element_type=jnp.float32)
    kept = lax.dynamic_slice_in_dim(partial, parity * 8, 8, 0)
    sent = lax.dynamic_slice_in_dim(partial, (1 - parity) * 8, 8, 0)
    arrived = lax.ppermute(sent, "gy", [(i, i ^ 1) for i in range(32)])
    mine = (kept + arrived).astype(jnp.bfloat16).reshape(16, 256)
    held, other = gather_planes(mine)
    gx = lax.axis_index("gx")
    spot = (gx % 2).astype(jnp.int32).reshape(1)
    part = translate(spot, offsets, held.reshape(4, 512, 256), other.reshape(4, 512, 256), m2l_ops)
    result = scatter_sums(part.reshape(8, 4, 16, 256))
    return result.reshape(1, 8, 2, 256)


def solution(mesh):
    return jax.shard_map(
        on_device,
        mesh=mesh,
        in_specs=(P("gx", "gy", None, None, None), P(), P("gy", None, None), P("gy", None)),
        out_specs=P("gx", "gy", None, None),
        check_vma=False,
    )
```

```python
import jax
import jax.numpy as jnp
from jax import lax
from jax.experimental import pallas as pl
from jax.experimental.pallas import tpu as pltpu
from jax.sharding import PartitionSpec as P

MESH = pl.DeviceIdType.MESH
def place():
    gx, gy = lax.axis_index("gx"), lax.axis_index("gy")
    return gx // 4, gx // 2 % 2, gx % 2, gy // 4, gy % 4


def device(x, zh, core, zl, y):
    return (x * 4 + zh * 2 + core, zl * 4 + y)


def greet(peers):
    barrier = pltpu.get_barrier_semaphore()
    for peer in peers:
        pl.semaphore_signal(barrier, inc=1, device_id=peer, device_id_type=MESH)
    pl.semaphore_wait(barrier, len(peers))


def source_offset(turn):
    return jnp.where(turn % 2 == 1, (turn + 1) // 2, (16 - turn // 2) % 16)


LAG = 4


def far_field_kernel(
    partial, offsets, operators, out,
    mine, arrived, held, other, ops, planes, total, part, from_y, summed, rounded, from_z,
    ops_sem, pair_send, pair_recv, z_send, z_recv, y_send, y_recv, x_send, x_recv, c_send, c_recv,
    sy_send, sy_recv, sz_send, sz_recv,
):
    x, zh, core, zl, y = place()
    zp = zh * 8 + zl
    parity = y % 2
    y_of = [(y + d) % 4 for d in (1, 2, 3)]
    x_peers = [device((x + d) % 4, zh, core, zl, y) for d in (1, 3)]
    y_peers = [device(x, zh, core, zl, to) for to in y_of]
    pair = device(x, zh, core, zl, y + 1 - 2 * parity)
    partner = device(x, zh, 1 - core, zl, y)

    def z_peer(offset):
        position = (zp + offset) % 16
        return device(x, position // 8, core, position % 8, y)

    def remote(src, dst, send, recv, target):
        return pltpu.make_async_remote_copy(
            src_ref=src, dst_ref=dst, send_sem=send, recv_sem=recv, device_id=target, device_id_type=MESH
        )

    def along_z(offset):
        to = (zp + offset) % 16
        return remote(mine, held.at[1 + core + zh - to // 8, zl, y], z_send.at[offset], z_recv.at[offset], z_peer(offset))

    def spot_of(turn):
        position = (zp + 16 - source_offset(turn)) % 16
        return position, 1 + core + position // 8 - zh, position % 8

    def along_y(turn, d):
        position, plane, row = spot_of(turn)
        piece = held.at[plane, row, y]
        return remote(piece, piece, y_send.at[position, d], y_recv.at[position, d], y_peers[d])

    def along_x(turn):
        position, plane, row = spot_of(turn)
        to = (x + jnp.where(plane >= 2, 1, 3)) % 4
        return remote(
            held.at[plane, row], held.at[(plane + 2) % 4, row], x_send.at[position], x_recv.at[position],
            device(to, zh, core, zl, y),
        )

    def across(turn, far):
        position, plane, row = spot_of(turn)
        plane = (plane + 2 * far) % 4
        return remote(held.at[plane, row], other.at[plane, row], c_send.at[position, far], c_recv.at[position, far], partner)

    fetch = pltpu.make_async_copy(operators, ops, ops_sem)
    fetch.start()
    greet([z_peer(d) for d in range(1, 16)] + y_peers + x_peers + [partner])

    swap = remote(partial.at[1 - parity], arrived, pair_send, pair_recv, pair)
    swap.start()
    swap.wait()
    coarse = (partial[parity] + arrived[...]).astype(jnp.bfloat16)
    mine[...] = coarse
    held[1 + core, zl, y] = coarse

    def send_z(turn, carry):
        along_z((16 - source_offset(turn)) % 16).start()
        return carry

    lax.fori_loop(1, 16, send_z, 0)

    def turns(turn, carry):
        @pl.when(turn < 16)
        def _():
            @pl.when(turn > 0)
            def _():
                along_z(source_offset(turn)).wait_recv()

            for d in range(3):
                along_y(turn, d).start()

        @pl.when((turn >= LAG) & (turn < 16 + LAG))
        def _():
            for d in range(3):
                along_y(turn - LAG, d).wait_recv()
            along_x(turn - LAG).start()
            across(turn - LAG, 0).start()

        @pl.when(turn >= 2 * LAG)
        def _():
            along_x(turn - 2 * LAG).wait_recv()
            across(turn - 2 * LAG, 1).start()

        return carry

    lax.fori_loop(0, 16 + 2 * LAG, turns, 0)

    def drain(turn, carry):
        @pl.when(turn > 0)
        def _():
            along_z(turn).wait_send()

        for d in range(3):
            along_y(turn, d).wait_send()
        along_x(turn).wait_send()
        across(turn, 0).wait()
        across(turn, 1).wait()
        return carry

    lax.fori_loop(0, 16, drain, 0)

    def widen(row, carry):
        for shift in range(-3, 4):
            for half in range(2):
                source = other if shift % 2 else held
                index = (shift + 3) // 2 if shift % 2 else (shift + 2) // 2 + core
                wide = source[index, row, 2 * half : 2 * half + 2].reshape(32, 256).astype(jnp.float32)
                for lanes in range(2):
                    piece = wide[:, lanes * 128 : lanes * 128 + 128]
                    planes[lanes, shift + 3, 2 * row + half, 0:32] = piece
                    planes[lanes, shift + 3, 2 * row + half, 32:64] = piece
        return carry

    lax.fori_loop(0, 8, widen, 0)
    total[...] = jnp.zeros_like(total)
    fetch.wait()

    def one(entry, carry):
        dx, dy, dz = offsets[entry * 3] + 3, offsets[entry * 3 + 1], offsets[entry * 3 + 2]
        start = 2 * ((dz + 16) % 16)
        halves = [
            jnp.concatenate([planes[lanes, dx, (line + dy + 16) % 16, pl.ds(start, 32), :] for line in range(16)], axis=0)
            for lanes in range(2)
        ]
        rolled = jnp.concatenate(halves, axis=1).astype(jnp.bfloat16)
        total[...] += jnp.dot(rolled, ops[entry], preferred_element_type=jnp.float32)
        return carry

    lax.fori_loop(0, 16, one, 0)
    part[...] = total[...].astype(jnp.bfloat16).reshape(8, 4, 16, 256)

    sums_y = [remote(part.at[:, y_of[d]], from_y.at[d], sy_send.at[d], sy_recv.at[d], y_peers[d]) for d in range(3)]
    for copy in sums_y:
        copy.start()
    for copy in sums_y:
        copy.wait()
    line = part[:, y].astype(jnp.float32)
    for d in range(3):
        line = line + from_y[d].astype(jnp.float32)
    summed[...] = line
    rounded[...] = line.astype(jnp.bfloat16)
    z_of = [(zl + d) % 8 for d in range(1, 8)]
    sums_z = [
        remote(rounded.at[z_of[d]], from_z.at[d], sz_send.at[d], sz_recv.at[d], device(x, zh, core, z_of[d], y))
        for d in range(7)
    ]
    for copy in sums_z:
        copy.start()
    for copy in sums_z:
        copy.wait()
    result = summed[zl]
    for d in range(7):
        result = result + from_z[d].astype(jnp.float32)
    out[...] = result


def far_field(partial, offsets, operators):
    dma, half = pltpu.SemaphoreType.DMA, jnp.bfloat16
    return pl.pallas_call(
        far_field_kernel,
        out_shape=jax.ShapeDtypeStruct((16, 256), jnp.float32),
        in_specs=[
            pl.BlockSpec(memory_space=pltpu.VMEM),
            pl.BlockSpec(memory_space=pltpu.SMEM),
            pl.BlockSpec(memory_space=pl.ANY),
        ],
        out_specs=pl.BlockSpec(memory_space=pltpu.VMEM),
        scratch_shapes=[
            pltpu.VMEM((16, 256), half),
            pltpu.VMEM((16, 256), jnp.float32),
            pltpu.VMEM((4, 8, 4, 16, 256), half),
            pltpu.VMEM((4, 8, 4, 16, 256), half),
            pltpu.VMEM((16, 256, 256), half),
            pltpu.VMEM((2, 7, 16, 64, 128), jnp.float32),
            pltpu.VMEM((512, 256), jnp.float32),
            pltpu.VMEM((8, 4, 16, 256), half),
            pltpu.VMEM((3, 8, 16, 256), half),
            pltpu.VMEM((8, 16, 256), jnp.float32),
            pltpu.VMEM((8, 16, 256), half),
            pltpu.VMEM((7, 16, 256), half),
            dma, dma, dma,
            dma((16,)), dma((16,)),
            dma((16, 3)), dma((16, 3)),
            dma((16,)), dma((16,)),
            dma((16, 2)), dma((16, 2)),
            dma((3,)), dma((3,)), dma((7,)), dma((7,)),
        ],
        compiler_params=pltpu.CompilerParams(collective_id=0, has_side_effects=True),
        name="far_field",
    )(partial, offsets, operators)


def on_device(fine_multipoles, m2m_ops, m2l_ops, offsets):
    parity = lax.axis_index("gy") % 2
    selected = lax.dynamic_index_in_dim(m2m_ops, parity, 1, keepdims=False)
    children = fine_multipoles[:, 0].reshape(2, 16, 2, 2, 256)
    partial = jnp.einsum("azcri,acio->zro", children, selected, preferred_element_type=jnp.float32)
    result = far_field(partial.reshape(2, 16, 256), offsets.reshape(-1), m2l_ops)
    return result.reshape(1, 8, 2, 256)


def solution(mesh):
    return jax.shard_map(
        on_device,
        mesh=mesh,
        in_specs=(P("gx", "gy", None, None, None), P(), P("gy", None, None), P("gy", None)),
        out_specs=P("gx", "gy", None, None),
        check_vma=False,
    )
```

```python
import jax
import jax.numpy as jnp
from jax import lax
from jax.experimental import pallas as pl
from jax.experimental.pallas import tpu as pltpu
from jax.sharding import PartitionSpec as P

MESH = pl.DeviceIdType.MESH
def place():
    gx, gy = lax.axis_index("gx"), lax.axis_index("gy")
    return gx // 4, gx // 2 % 2, gx % 2, gy // 4, gy % 4


def device(x, zh, core, zl, y):
    return (x * 4 + zh * 2 + core, zl * 4 + y)


def greet(peers):
    barrier = pltpu.get_barrier_semaphore()
    for peer in peers:
        pl.semaphore_signal(barrier, inc=1, device_id=peer, device_id_type=MESH)


def child_rows(child):
    to = lax.broadcasted_iota(jnp.int32, (32, 64), 0)
    source = lax.broadcasted_iota(jnp.int32, (32, 64), 1)
    return jnp.where(source == to // 2 * 4 + child * 2 + to % 2, 1.0, 0.0).astype(jnp.bfloat16)


def source_offset(turn):
    return jnp.where(turn % 2 == 1, (turn + 1) // 2, (16 - turn // 2) % 16)


LAG = 4


def far_field_kernel(
    fine, upward, offsets, operators, out,
    up, partial, mine, arrived, held, other, ops, planes, total, part, from_y, summed, rounded, from_z,
    ops_sem, up_sem, pair_send, pair_recv, z_send, z_recv, y_send, y_recv, x_send, x_recv, c_send, c_recv,
    sy_send, sy_recv, sz_send, sz_recv,
):
    x, zh, core, zl, y = place()
    zp = zh * 8 + zl
    parity = y % 2
    y_of = [(y + d) % 4 for d in (1, 2, 3)]
    x_peers = [device((x + d) % 4, zh, core, zl, y) for d in (1, 3)]
    y_peers = [device(x, zh, core, zl, to) for to in y_of]
    pair = device(x, zh, core, zl, y + 1 - 2 * parity)
    partner = device(x, zh, 1 - core, zl, y)

    def z_peer(offset):
        position = (zp + offset) % 16
        return device(x, position // 8, core, position % 8, y)

    def remote(src, dst, send, recv, target):
        return pltpu.make_async_remote_copy(
            src_ref=src, dst_ref=dst, send_sem=send, recv_sem=recv, device_id=target, device_id_type=MESH
        )

    def along_z(offset):
        to = (zp + offset) % 16
        return remote(mine, held.at[1 + core + zh - to // 8, zl, y], z_send.at[offset], z_recv.at[offset], z_peer(offset))

    def spot_of(turn):
        position = (zp + 16 - source_offset(turn)) % 16
        return position, 1 + core + position // 8 - zh, position % 8

    def along_y(turn, d):
        position, plane, row = spot_of(turn)
        piece = held.at[plane, row, y]
        return remote(piece, piece, y_send.at[position, d], y_recv.at[position, d], y_peers[d])

    def along_x(turn):
        position, plane, row = spot_of(turn)
        to = (x + jnp.where(plane >= 2, 1, 3)) % 4
        return remote(
            held.at[plane, row], held.at[(plane + 2) % 4, row], x_send.at[position], x_recv.at[position],
            device(to, zh, core, zl, y),
        )

    def across(turn, far):
        position, plane, row = spot_of(turn)
        plane = (plane + 2 * far) % 4
        return remote(held.at[plane, row], other.at[plane, row], c_send.at[position, far], c_recv.at[position, far], partner)

    peers = [z_peer(d) for d in range(1, 16)] + y_peers + x_peers + [partner]
    greet(peers)
    lift = pltpu.make_async_copy(upward.at[:, parity], up, up_sem)
    lift.start()
    fetch = pltpu.make_async_copy(operators, ops, ops_sem)
    fetch.start()
    picked = [
        jnp.dot(child_rows(c), fine[a, 0].reshape(64, 256), preferred_element_type=jnp.float32).astype(jnp.bfloat16)
        for a in range(2)
        for c in range(2)
    ]
    lift.wait()
    terms = [jnp.dot(picked[n], up[n // 2, n % 2], preferred_element_type=jnp.float32) for n in range(4)]
    partial[...] = ((terms[0] + terms[1]) + (terms[2] + terms[3])).reshape(2, 16, 256)
    pl.semaphore_wait(pltpu.get_barrier_semaphore(), len(peers))

    swap = remote(partial.at[1 - parity], arrived, pair_send, pair_recv, pair)
    swap.start()
    swap.wait()
    coarse = (partial[parity] + arrived[...]).astype(jnp.bfloat16)
    mine[...] = coarse
    held[1 + core, zl, y] = coarse

    def send_z(turn, carry):
        along_z((16 - source_offset(turn)) % 16).start()
        return carry

    lax.fori_loop(1, 16, send_z, 0)

    def turns(turn, carry):
        @pl.when(turn < 16)
        def _():
            @pl.when(turn > 0)
            def _():
                along_z(source_offset(turn)).wait_recv()

            for d in range(3):
                along_y(turn, d).start()

        @pl.when((turn >= LAG) & (turn < 16 + LAG))
        def _():
            for d in range(3):
                along_y(turn - LAG, d).wait_recv()
            along_x(turn - LAG).start()
            across(turn - LAG, 0).start()

        @pl.when(turn >= 2 * LAG)
        def _():
            along_x(turn - 2 * LAG).wait_recv()
            across(turn - 2 * LAG, 1).start()

        return carry

    lax.fori_loop(0, 16 + 2 * LAG, turns, 0)

    def drain(turn, carry):
        @pl.when(turn > 0)
        def _():
            along_z(turn).wait_send()

        for d in range(3):
            along_y(turn, d).wait_send()
        along_x(turn).wait_send()
        across(turn, 0).wait()
        across(turn, 1).wait()
        return carry

    lax.fori_loop(0, 16, drain, 0)

    def widen(row, carry):
        for shift in range(-3, 4):
            for half in range(2):
                source = other if shift % 2 else held
                index = (shift + 3) // 2 if shift % 2 else (shift + 2) // 2 + core
                wide = source[index, row, 2 * half : 2 * half + 2].reshape(32, 256).astype(jnp.float32)
                for lanes in range(2):
                    piece = wide[:, lanes * 128 : lanes * 128 + 128]
                    planes[lanes, shift + 3, 2 * row + half, 0:32] = piece
                    planes[lanes, shift + 3, 2 * row + half, 32:64] = piece
        return carry

    lax.fori_loop(0, 8, widen, 0)
    total[...] = jnp.zeros_like(total)
    fetch.wait()

    def one(entry, carry):
        dx, dy, dz = offsets[0, entry] + 3, offsets[1, entry], offsets[2, entry]
        start = 2 * ((dz + 16) % 16)
        halves = [
            jnp.concatenate([planes[lanes, dx, (line + dy + 16) % 16, pl.ds(start, 32), :] for line in range(16)], axis=0)
            for lanes in range(2)
        ]
        rolled = jnp.concatenate(halves, axis=1).astype(jnp.bfloat16)
        total[...] += jnp.dot(rolled, ops[entry], preferred_element_type=jnp.float32)
        return carry

    lax.fori_loop(0, 16, one, 0)
    part[...] = total[...].astype(jnp.bfloat16).reshape(8, 4, 16, 256)

    sums_y = [remote(part.at[:, y_of[d]], from_y.at[d], sy_send.at[d], sy_recv.at[d], y_peers[d]) for d in range(3)]
    for copy in sums_y:
        copy.start()
    for copy in sums_y:
        copy.wait()
    line = part[:, y].astype(jnp.float32)
    for d in range(3):
        line = line + from_y[d].astype(jnp.float32)
    summed[...] = line
    rounded[...] = line.astype(jnp.bfloat16)
    z_of = [(zl + d) % 8 for d in range(1, 8)]
    sums_z = [
        remote(rounded.at[z_of[d]], from_z.at[d], sz_send.at[d], sz_recv.at[d], device(x, zh, core, z_of[d], y))
        for d in range(7)
    ]
    for copy in sums_z:
        copy.start()
    for copy in sums_z:
        copy.wait()
    result = summed[zl]
    for d in range(7):
        result = result + from_z[d].astype(jnp.float32)
    out[...] = result.reshape(1, 8, 2, 256)


def far_field(fine, upward, offsets, operators):
    dma, half = pltpu.SemaphoreType.DMA, jnp.bfloat16
    return pl.pallas_call(
        far_field_kernel,
        out_shape=jax.ShapeDtypeStruct((1, 8, 2, 256), jnp.float32),
        in_specs=[
            pl.BlockSpec(memory_space=pltpu.VMEM),
            pl.BlockSpec(memory_space=pl.ANY),
            pl.BlockSpec(memory_space=pltpu.SMEM),
            pl.BlockSpec(memory_space=pl.ANY),
        ],
        out_specs=pl.BlockSpec(memory_space=pltpu.VMEM),
        scratch_shapes=[
            pltpu.VMEM((2, 2, 256, 256), half),
            pltpu.VMEM((2, 16, 256), jnp.float32),
            pltpu.VMEM((16, 256), half),
            pltpu.VMEM((16, 256), jnp.float32),
            pltpu.VMEM((4, 8, 4, 16, 256), half),
            pltpu.VMEM((4, 8, 4, 16, 256), half),
            pltpu.VMEM((16, 256, 256), half),
            pltpu.VMEM((2, 7, 16, 64, 128), jnp.float32),
            pltpu.VMEM((512, 256), jnp.float32),
            pltpu.VMEM((8, 4, 16, 256), half),
            pltpu.VMEM((3, 8, 16, 256), half),
            pltpu.VMEM((8, 16, 256), jnp.float32),
            pltpu.VMEM((8, 16, 256), half),
            pltpu.VMEM((7, 16, 256), half),
            dma, dma, dma, dma,
            dma((16,)), dma((16,)),
            dma((16, 3)), dma((16, 3)),
            dma((16,)), dma((16,)),
            dma((16, 2)), dma((16, 2)),
            dma((3,)), dma((3,)), dma((7,)), dma((7,)),
        ],
        compiler_params=pltpu.CompilerParams(collective_id=0, has_side_effects=True),
        name="far_field",
    )(fine, upward, offsets, operators)


def on_device(fine_multipoles, m2m_ops, m2l_ops, offsets):
    return far_field(fine_multipoles, m2m_ops, offsets.T, m2l_ops)


def solution(mesh):
    return jax.shard_map(
        on_device,
        mesh=mesh,
        in_specs=(P("gx", "gy", None, None, None), P(), P("gy", None, None), P("gy", None)),
        out_specs=P("gx", "gy", None, None),
        check_vma=False,
    )
```

```python
import jax
import jax.numpy as jnp
from jax import lax
from jax.experimental import pallas as pl
from jax.experimental.pallas import tpu as pltpu
from jax.sharding import PartitionSpec as P

MESH = pl.DeviceIdType.MESH
def place():
    gx, gy = lax.axis_index("gx"), lax.axis_index("gy")
    return gx // 4, gx // 2 % 2, gx % 2, gy // 4, gy % 4


def device(x, zh, core, zl, y):
    return (x * 4 + zh * 2 + core, zl * 4 + y)


def greet(peers):
    barrier = pltpu.get_barrier_semaphore()
    for peer in peers:
        pl.semaphore_signal(barrier, inc=1, device_id=peer, device_id_type=MESH)


def child_rows(child):
    to = lax.broadcasted_iota(jnp.int32, (32, 64), 0)
    source = lax.broadcasted_iota(jnp.int32, (32, 64), 1)
    return jnp.where(source == to // 2 * 4 + child * 2 + to % 2, 1.0, 0.0).astype(jnp.bfloat16)


def source_offset(turn):
    return jnp.where(turn % 2 == 1, (turn + 1) // 2, (16 - turn // 2) % 16)


Y_LAG, X_LAG = 12, 8


def far_field_kernel(
    fine, upward, offsets, operators, out,
    up, partial, mine, arrived, held, other, ops, planes, total, part, from_y, summed, rounded, from_z,
    ops_sem, up_sem, pair_send, pair_recv, z_send, z_recv, y_send, y_recv, x_send, x_recv, c_send, c_recv,
    sy_send, sy_recv, sz_send, sz_recv,
):
    x, zh, core, zl, y = place()
    zp = zh * 8 + zl
    parity = y % 2
    y_of = [(y + d) % 4 for d in (1, 2, 3)]
    x_peers = [device((x + d) % 4, zh, core, zl, y) for d in (1, 3)]
    y_peers = [device(x, zh, core, zl, to) for to in y_of]
    pair = device(x, zh, core, zl, y + 1 - 2 * parity)
    partner = device(x, zh, 1 - core, zl, y)

    def z_peer(offset):
        position = (zp + offset) % 16
        return device(x, position // 8, core, position % 8, y)

    def remote(src, dst, send, recv, target):
        return pltpu.make_async_remote_copy(
            src_ref=src, dst_ref=dst, send_sem=send, recv_sem=recv, device_id=target, device_id_type=MESH
        )

    def along_z(offset):
        to = (zp + offset) % 16
        return remote(mine, held.at[1 + core + zh - to // 8, zl, y], z_send.at[offset], z_recv.at[offset], z_peer(offset))

    def spot_of(turn):
        position = (zp + 16 - source_offset(turn)) % 16
        return position, 1 + core + position // 8 - zh, position % 8

    def along_y(turn, d):
        position, plane, row = spot_of(turn)
        piece = held.at[plane, row, y]
        return remote(piece, piece, y_send.at[position, d], y_recv.at[position, d], y_peers[d])

    def along_x(turn):
        position, plane, row = spot_of(turn)
        to = (x + jnp.where(plane >= 2, 1, 3)) % 4
        return remote(
            held.at[plane, row], held.at[(plane + 2) % 4, row], x_send.at[position], x_recv.at[position],
            device(to, zh, core, zl, y),
        )

    def across(turn, far):
        position, plane, row = spot_of(turn)
        plane = (plane + 2 * far) % 4
        return remote(held.at[plane, row], other.at[plane, row], c_send.at[position, far], c_recv.at[position, far], partner)

    peers = [z_peer(d) for d in range(1, 16)] + y_peers + x_peers + [partner]
    greet(peers)
    lift = pltpu.make_async_copy(upward.at[:, parity], up, up_sem)
    lift.start()
    fetch = pltpu.make_async_copy(operators, ops, ops_sem)
    fetch.start()
    picked = [
        jnp.dot(child_rows(c), fine[a, 0].reshape(64, 256), preferred_element_type=jnp.float32).astype(jnp.bfloat16)
        for a in range(2)
        for c in range(2)
    ]
    lift.wait()
    terms = [jnp.dot(picked[n], up[n // 2, n % 2], preferred_element_type=jnp.float32) for n in range(4)]
    partial[...] = ((terms[0] + terms[1]) + (terms[2] + terms[3])).reshape(2, 16, 256)
    pl.semaphore_wait(pltpu.get_barrier_semaphore(), len(peers))

    swap = remote(partial.at[1 - parity], arrived, pair_send, pair_recv, pair)
    swap.start()
    swap.wait()
    coarse = (partial[parity] + arrived[...]).astype(jnp.bfloat16)
    mine[...] = coarse
    held[1 + core, zl, y] = coarse

    def send_z(turn, carry):
        along_z((16 - source_offset(turn)) % 16).start()
        return carry

    lax.fori_loop(1, 16, send_z, 0)

    def turns(turn, carry):
        @pl.when(turn < 16)
        def _():
            @pl.when(turn > 0)
            def _():
                along_z(source_offset(turn)).wait_recv()

            for d in range(3):
                along_y(turn, d).start()

        @pl.when((turn >= Y_LAG) & (turn < 16 + Y_LAG))
        def _():
            for d in range(3):
                along_y(turn - Y_LAG, d).wait_recv()
            along_x(turn - Y_LAG).start()
            across(turn - Y_LAG, 0).start()

        @pl.when(turn >= Y_LAG + X_LAG)
        def _():
            along_x(turn - Y_LAG - X_LAG).wait_recv()
            across(turn - Y_LAG - X_LAG, 1).start()

        return carry

    lax.fori_loop(0, 16 + Y_LAG + X_LAG, turns, 0)

    def drain(turn, carry):
        @pl.when(turn > 0)
        def _():
            along_z(turn).wait_send()

        for d in range(3):
            along_y(turn, d).wait_send()
        along_x(turn).wait_send()
        across(turn, 0).wait()
        across(turn, 1).wait()
        return carry

    lax.fori_loop(0, 16, drain, 0)

    def widen(row, carry):
        for shift in range(-3, 4):
            for half in range(2):
                source = other if shift % 2 else held
                index = (shift + 3) // 2 if shift % 2 else (shift + 2) // 2 + core
                wide = source[index, row, 2 * half : 2 * half + 2].reshape(32, 256).astype(jnp.float32)
                for lanes in range(2):
                    piece = wide[:, lanes * 128 : lanes * 128 + 128]
                    planes[lanes, shift + 3, 2 * row + half, 0:32] = piece
                    planes[lanes, shift + 3, 2 * row + half, 32:64] = piece
        return carry

    lax.fori_loop(0, 8, widen, 0)
    fetch.wait()

    def half_sums(odd):
        total[...] = jnp.zeros_like(total)

        def one(entry, carry):
            dx, dy, dz = offsets[0, entry] + 3, offsets[1, entry], offsets[2, entry]
            start = 2 * ((dz + 16) % 16)
            halves = [
                jnp.concatenate(
                    [planes[lanes, dx, (2 * row + odd + dy + 16) % 16, pl.ds(start, 32), :] for row in range(8)], axis=0
                )
                for lanes in range(2)
            ]
            rolled = jnp.concatenate(halves, axis=1).astype(jnp.bfloat16)
            total[...] += jnp.dot(rolled, ops[entry], preferred_element_type=jnp.float32)
            return carry

        lax.fori_loop(0, 16, one, 0)
        part[:, pl.ds(2 * odd, 2)] = total[...].astype(jnp.bfloat16).reshape(8, 2, 16, 256)

    def sum_to(to):
        slot = (to + 3 - y) % 4
        return remote(
            part.at[:, to], from_y.at[slot], sy_send.at[slot], sy_recv.at[slot], device(x, zh, core, zl, to)
        )

    first = 1 - y // 2
    half_sums(first)
    sum_to(2 * first).start()
    sum_to(2 * first + 1).start()
    half_sums(1 - first)
    sum_to(y + 1 - 2 * parity).start()
    sums_y = [sum_to(to) for to in y_of]
    for copy in sums_y:
        copy.wait()
    line = part[:, y].astype(jnp.float32)
    for d in range(3):
        line = line + from_y[d].astype(jnp.float32)
    summed[...] = line
    rounded[...] = line.astype(jnp.bfloat16)
    z_of = [(zl + d) % 8 for d in range(1, 8)]
    sums_z = [
        remote(rounded.at[z_of[d]], from_z.at[d], sz_send.at[d], sz_recv.at[d], device(x, zh, core, z_of[d], y))
        for d in range(7)
    ]
    for copy in sums_z:
        copy.start()
    for copy in sums_z:
        copy.wait()
    result = summed[zl]
    for d in range(7):
        result = result + from_z[d].astype(jnp.float32)
    out[...] = result.reshape(1, 8, 2, 256)


def far_field(fine, upward, offsets, operators):
    dma, half = pltpu.SemaphoreType.DMA, jnp.bfloat16
    return pl.pallas_call(
        far_field_kernel,
        out_shape=jax.ShapeDtypeStruct((1, 8, 2, 256), jnp.float32),
        in_specs=[
            pl.BlockSpec(memory_space=pltpu.VMEM),
            pl.BlockSpec(memory_space=pl.ANY),
            pl.BlockSpec(memory_space=pltpu.SMEM),
            pl.BlockSpec(memory_space=pl.ANY),
        ],
        out_specs=pl.BlockSpec(memory_space=pltpu.VMEM),
        scratch_shapes=[
            pltpu.VMEM((2, 2, 256, 256), half),
            pltpu.VMEM((2, 16, 256), jnp.float32),
            pltpu.VMEM((16, 256), half),
            pltpu.VMEM((16, 256), jnp.float32),
            pltpu.VMEM((4, 8, 4, 16, 256), half),
            pltpu.VMEM((4, 8, 4, 16, 256), half),
            pltpu.VMEM((16, 256, 256), half),
            pltpu.VMEM((2, 7, 16, 64, 128), jnp.float32),
            pltpu.VMEM((256, 256), jnp.float32),
            pltpu.VMEM((8, 4, 16, 256), half),
            pltpu.VMEM((3, 8, 16, 256), half),
            pltpu.VMEM((8, 16, 256), jnp.float32),
            pltpu.VMEM((8, 16, 256), half),
            pltpu.VMEM((7, 16, 256), half),
            dma, dma, dma, dma,
            dma((16,)), dma((16,)),
            dma((16, 3)), dma((16, 3)),
            dma((16,)), dma((16,)),
            dma((16, 2)), dma((16, 2)),
            dma((3,)), dma((3,)), dma((7,)), dma((7,)),
        ],
        compiler_params=pltpu.CompilerParams(collective_id=0, has_side_effects=True),
        name="far_field",
    )(fine, upward, offsets, operators)


def on_device(fine_multipoles, m2m_ops, m2l_ops, offsets):
    return far_field(fine_multipoles, m2m_ops, offsets.T, m2l_ops)


def solution(mesh):
    return jax.shard_map(
        on_device,
        mesh=mesh,
        in_specs=(P("gx", "gy", None, None, None), P(), P("gy", None, None), P("gy", None)),
        out_specs=P("gx", "gy", None, None),
        check_vma=False,
    )
```

```python
import jax
import jax.numpy as jnp
from jax import lax
from jax.experimental import pallas as pl
from jax.experimental.pallas import tpu as pltpu
from jax.sharding import PartitionSpec as P

MESH = pl.DeviceIdType.MESH
def place():
    gx, gy = lax.axis_index("gx"), lax.axis_index("gy")
    return gx // 4, gx // 2 % 2, gx % 2, gy // 4, gy % 4


def device(x, zh, core, zl, y):
    return (x * 4 + zh * 2 + core, zl * 4 + y)


def greet(peers):
    barrier = pltpu.get_barrier_semaphore()
    for peer in peers:
        pl.semaphore_signal(barrier, inc=1, device_id=peer, device_id_type=MESH)


def child_rows(child):
    to = lax.broadcasted_iota(jnp.int32, (32, 64), 0)
    source = lax.broadcasted_iota(jnp.int32, (32, 64), 1)
    return jnp.where(source == to // 2 * 4 + child * 2 + to % 2, 1.0, 0.0).astype(jnp.bfloat16)


def source_offset(turn):
    return jnp.where(turn % 2 == 1, (turn + 1) // 2, (16 - turn // 2) % 16)


Y_LAG, X_LAG = 9, 12


def far_field_kernel(
    fine, upward, offsets, operators, out,
    up, partial, mine, arrived, held, other, ops, planes, total, part, from_y, summed, rounded, from_z,
    ops_sem, up_sem, pair_send, pair_recv, z_send, z_recv, y_send, y_recv, x_send, x_recv, c_send, c_recv,
    sy_send, sy_recv, sz_send, sz_recv,
):
    x, zh, core, zl, y = place()
    zp = zh * 8 + zl
    parity = y % 2
    y_of = [(y + d) % 4 for d in (1, 2, 3)]
    x_peers = [device((x + d) % 4, zh, core, zl, y) for d in (1, 3)]
    y_peers = [device(x, zh, core, zl, to) for to in y_of]
    pair = device(x, zh, core, zl, y + 1 - 2 * parity)
    partner = device(x, zh, 1 - core, zl, y)

    def z_peer(offset):
        position = (zp + offset) % 16
        return device(x, position // 8, core, position % 8, y)

    def remote(src, dst, send, recv, target):
        return pltpu.make_async_remote_copy(
            src_ref=src, dst_ref=dst, send_sem=send, recv_sem=recv, device_id=target, device_id_type=MESH
        )

    def along_z(offset):
        to = (zp + offset) % 16
        return remote(mine, held.at[1 + core + zh - to // 8, zl, y], z_send.at[offset], z_recv.at[offset], z_peer(offset))

    def spot_of(turn):
        position = (zp + 16 - source_offset(turn)) % 16
        return position, 1 + core + position // 8 - zh, position % 8

    def along_y(turn, d):
        position, plane, row = spot_of(turn)
        piece = held.at[plane, row, y]
        return remote(piece, piece, y_send.at[position, d], y_recv.at[position, d], y_peers[d])

    def along_x(turn):
        position, plane, row = spot_of(turn)
        to = (x + jnp.where(plane >= 2, 1, 3)) % 4
        return remote(
            held.at[plane, row], held.at[(plane + 2) % 4, row], x_send.at[position], x_recv.at[position],
            device(to, zh, core, zl, y),
        )

    def across(turn, far):
        position, plane, row = spot_of(turn)
        plane = (plane + 2 * far) % 4
        return remote(held.at[plane, row], other.at[plane, row], c_send.at[position, far], c_recv.at[position, far], partner)

    peers = [z_peer(d) for d in range(1, 16)] + y_peers + x_peers + [partner]
    greet(peers)
    lift = pltpu.make_async_copy(upward.at[:, parity], up, up_sem)
    lift.start()
    fetch = pltpu.make_async_copy(operators, ops, ops_sem)
    fetch.start()
    picked = [
        jnp.dot(child_rows(c), fine[a, 0].reshape(64, 256), preferred_element_type=jnp.float32).astype(jnp.bfloat16)
        for a in range(2)
        for c in range(2)
    ]
    lift.wait()
    terms = [jnp.dot(picked[n], up[n // 2, n % 2], preferred_element_type=jnp.float32) for n in range(4)]
    partial[...] = ((terms[0] + terms[1]) + (terms[2] + terms[3])).reshape(2, 16, 256)
    pl.semaphore_wait(pltpu.get_barrier_semaphore(), len(peers))

    swap = remote(partial.at[1 - parity], arrived, pair_send, pair_recv, pair)
    swap.start()
    swap.wait()
    coarse = (partial[parity] + arrived[...]).astype(jnp.bfloat16)
    mine[...] = coarse
    held[1 + core, zl, y] = coarse

    def send_z(turn, carry):
        along_z((16 - source_offset(turn)) % 16).start()
        return carry

    lax.fori_loop(1, 16, send_z, 0)

    def turns(turn, carry):
        @pl.when(turn < 16)
        def _():
            @pl.when(turn > 0)
            def _():
                along_z(source_offset(turn)).wait_recv()

            for d in range(3):
                along_y(turn, d).start()

        @pl.when((turn >= Y_LAG) & (turn < 16 + Y_LAG))
        def _():
            for d in range(3):
                along_y(turn - Y_LAG, d).wait_recv()
            along_x(turn - Y_LAG).start()
            across(turn - Y_LAG, 0).start()

        @pl.when(turn >= Y_LAG + X_LAG)
        def _():
            along_x(turn - Y_LAG - X_LAG).wait_recv()
            across(turn - Y_LAG - X_LAG, 1).start()

        return carry

    lax.fori_loop(0, 16 + Y_LAG + X_LAG, turns, 0)

    def widen(shifts):
        def one_row(row, carry):
            for shift in shifts:
                for half in range(2):
                    source = other if shift % 2 else held
                    index = (shift + 3) // 2 if shift % 2 else (shift + 2) // 2 + core
                    wide = source[index, row, 2 * half : 2 * half + 2].reshape(32, 256).astype(jnp.float32)
                    for lanes in range(2):
                        piece = wide[:, lanes * 128 : lanes * 128 + 128]
                        planes[lanes, shift + 3, 2 * row + half, 0:32] = piece
                        planes[lanes, shift + 3, 2 * row + half, 32:64] = piece
            return carry

        lax.fori_loop(0, 8, one_row, 0)

    widen((-2, 0, 2))

    def drain(turn, carry):
        @pl.when(turn > 0)
        def _():
            along_z(turn).wait_send()

        for d in range(3):
            along_y(turn, d).wait_send()
        along_x(turn).wait_send()
        across(turn, 0).wait()
        across(turn, 1).wait()
        return carry

    lax.fori_loop(0, 16, drain, 0)

    widen((-3, -1, 1, 3))
    fetch.wait()

    def half_sums(odd):
        total[...] = jnp.zeros_like(total)

        def one(entry, carry):
            dx, dy, dz = offsets[0, entry] + 3, offsets[1, entry], offsets[2, entry]
            start = 2 * ((dz + 16) % 16)
            halves = [
                jnp.concatenate(
                    [planes[lanes, dx, (2 * row + odd + dy + 16) % 16, pl.ds(start, 32), :] for row in range(8)], axis=0
                )
                for lanes in range(2)
            ]
            rolled = jnp.concatenate(halves, axis=1).astype(jnp.bfloat16)
            total[...] += jnp.dot(rolled, ops[entry], preferred_element_type=jnp.float32)
            return carry

        lax.fori_loop(0, 16, one, 0)
        part[:, pl.ds(2 * odd, 2)] = total[...].astype(jnp.bfloat16).reshape(8, 2, 16, 256)

    def sum_to(to):
        slot = (to + 3 - y) % 4
        return remote(
            part.at[:, to], from_y.at[slot], sy_send.at[slot], sy_recv.at[slot], device(x, zh, core, zl, to)
        )

    first = 1 - y // 2
    half_sums(first)
    sum_to(2 * first).start()
    sum_to(2 * first + 1).start()
    half_sums(1 - first)
    sum_to(y + 1 - 2 * parity).start()
    sums_y = [sum_to(to) for to in y_of]
    for copy in sums_y:
        copy.wait()
    line = part[:, y].astype(jnp.float32)
    for d in range(3):
        line = line + from_y[d].astype(jnp.float32)
    summed[...] = line
    rounded[...] = line.astype(jnp.bfloat16)
    z_of = [(zl + d) % 8 for d in range(1, 8)]
    sums_z = [
        remote(rounded.at[z_of[d]], from_z.at[d], sz_send.at[d], sz_recv.at[d], device(x, zh, core, z_of[d], y))
        for d in range(7)
    ]
    for copy in sums_z:
        copy.start()
    for copy in sums_z:
        copy.wait()
    result = summed[zl]
    for d in range(7):
        result = result + from_z[d].astype(jnp.float32)
    out[...] = result.reshape(1, 8, 2, 256)


def far_field(fine, upward, offsets, operators):
    dma, half = pltpu.SemaphoreType.DMA, jnp.bfloat16
    return pl.pallas_call(
        far_field_kernel,
        out_shape=jax.ShapeDtypeStruct((1, 8, 2, 256), jnp.float32),
        in_specs=[
            pl.BlockSpec(memory_space=pltpu.VMEM),
            pl.BlockSpec(memory_space=pl.ANY),
            pl.BlockSpec(memory_space=pltpu.SMEM),
            pl.BlockSpec(memory_space=pl.ANY),
        ],
        out_specs=pl.BlockSpec(memory_space=pltpu.VMEM),
        scratch_shapes=[
            pltpu.VMEM((2, 2, 256, 256), half),
            pltpu.VMEM((2, 16, 256), jnp.float32),
            pltpu.VMEM((16, 256), half),
            pltpu.VMEM((16, 256), jnp.float32),
            pltpu.VMEM((4, 8, 4, 16, 256), half),
            pltpu.VMEM((4, 8, 4, 16, 256), half),
            pltpu.VMEM((16, 256, 256), half),
            pltpu.VMEM((2, 7, 16, 64, 128), jnp.float32),
            pltpu.VMEM((256, 256), jnp.float32),
            pltpu.VMEM((8, 4, 16, 256), half),
            pltpu.VMEM((3, 8, 16, 256), half),
            pltpu.VMEM((8, 16, 256), jnp.float32),
            pltpu.VMEM((8, 16, 256), half),
            pltpu.VMEM((7, 16, 256), half),
            dma, dma, dma, dma,
            dma((16,)), dma((16,)),
            dma((16, 3)), dma((16, 3)),
            dma((16,)), dma((16,)),
            dma((16, 2)), dma((16, 2)),
            dma((3,)), dma((3,)), dma((7,)), dma((7,)),
        ],
        compiler_params=pltpu.CompilerParams(collective_id=0, has_side_effects=True),
        name="far_field",
    )(fine, upward, offsets, operators)


def on_device(fine_multipoles, m2m_ops, m2l_ops, offsets):
    return far_field(fine_multipoles, m2m_ops, offsets.T, m2l_ops)


def solution(mesh):
    return jax.shard_map(
        on_device,
        mesh=mesh,
        in_specs=(P("gx", "gy", None, None, None), P(), P("gy", None, None), P("gy", None)),
        out_specs=P("gx", "gy", None, None),
        check_vma=False,
    )
```

```python
import jax
import jax.numpy as jnp
from jax import lax
from jax.experimental import pallas as pl
from jax.experimental.pallas import tpu as pltpu
from jax.sharding import PartitionSpec as P

MESH = pl.DeviceIdType.MESH
def place():
    gx, gy = lax.axis_index("gx"), lax.axis_index("gy")
    return gx // 4, gx // 2 % 2, gx % 2, gy // 4, gy % 4


def device(x, zh, core, zl, y):
    return (x * 4 + zh * 2 + core, zl * 4 + y)


def greet(peers):
    barrier = pltpu.get_barrier_semaphore()
    for peer in peers:
        pl.semaphore_signal(barrier, inc=1, device_id=peer, device_id_type=MESH)


def child_rows(child):
    to = lax.broadcasted_iota(jnp.int32, (32, 64), 0)
    source = lax.broadcasted_iota(jnp.int32, (32, 64), 1)
    return jnp.where(source == to // 2 * 4 + child * 2 + to % 2, 1.0, 0.0).astype(jnp.bfloat16)


def source_offset(turn):
    return jnp.where(turn % 2 == 1, (turn + 1) // 2, (16 - turn // 2) % 16)


Y_LAG, X_LAG = 9, 12


def far_field_kernel(
    fine, upward, offsets, operators, out,
    up, partial, mine, arrived, held, other, ops, planes, total, part, from_y, summed, rounded, from_z,
    ops_sem, up_sem, pair_send, pair_recv, z_send, z_recv, y_send, y_recv, x_send, x_recv, c_send, c_recv,
    sy_send, sy_recv, sz_send, sz_recv,
):
    x, zh, core, zl, y = place()
    zp = zh * 8 + zl
    parity = y % 2
    y_of = [(y + d) % 4 for d in (1, 2, 3)]
    x_peers = [device((x + d) % 4, zh, core, zl, y) for d in (1, 3)]
    y_peers = [device(x, zh, core, zl, to) for to in y_of]
    pair = device(x, zh, core, zl, y + 1 - 2 * parity)
    partner = device(x, zh, 1 - core, zl, y)

    def z_peer(offset):
        position = (zp + offset) % 16
        return device(x, position // 8, core, position % 8, y)

    def remote(src, dst, send, recv, target):
        return pltpu.make_async_remote_copy(
            src_ref=src, dst_ref=dst, send_sem=send, recv_sem=recv, device_id=target, device_id_type=MESH
        )

    def along_z(offset):
        to = (zp + offset) % 16
        return remote(mine, held.at[1 + core + zh - to // 8, zl, y], z_send.at[offset], z_recv.at[offset], z_peer(offset))

    def spot_of(turn):
        position = (zp + 16 - source_offset(turn)) % 16
        return position, 1 + core + position // 8 - zh, position % 8

    def along_y(turn, d):
        position, plane, row = spot_of(turn)
        piece = held.at[plane, row, y]
        return remote(piece, piece, y_send.at[position, d], y_recv.at[position, d], y_peers[d])

    def along_x(turn):
        position, plane, row = spot_of(turn)
        to = (x + jnp.where(plane >= 2, 1, 3)) % 4
        return remote(
            held.at[plane, row], held.at[(plane + 2) % 4, row], x_send.at[position], x_recv.at[position],
            device(to, zh, core, zl, y),
        )

    def across(turn, far):
        position, plane, row = spot_of(turn)
        plane = (plane + 2 * far) % 4
        return remote(held.at[plane, row], other.at[plane, row], c_send.at[position, far], c_recv.at[position, far], partner)

    peers = [z_peer(d) for d in range(1, 16)] + y_peers + x_peers + [partner]
    greet(peers)
    lift = pltpu.make_async_copy(upward.at[:, parity], up, up_sem)
    lift.start()
    fetch = pltpu.make_async_copy(operators, ops, ops_sem)
    fetch.start()
    picked = [
        jnp.dot(child_rows(c), fine[a, 0].reshape(64, 256), preferred_element_type=jnp.float32).astype(jnp.bfloat16)
        for a in range(2)
        for c in range(2)
    ]
    lift.wait()
    terms = [jnp.dot(picked[n], up[n // 2, n % 2], preferred_element_type=jnp.float32) for n in range(4)]
    partial[...] = ((terms[0] + terms[1]) + (terms[2] + terms[3])).reshape(2, 16, 256)
    pl.semaphore_wait(pltpu.get_barrier_semaphore(), len(peers))

    swap = remote(partial.at[1 - parity], arrived, pair_send, pair_recv, pair)
    swap.start()
    swap.wait()
    coarse = (partial[parity] + arrived[...]).astype(jnp.bfloat16)
    mine[...] = coarse
    held[1 + core, zl, y] = coarse

    def send_z(turn, carry):
        along_z((16 - source_offset(turn)) % 16).start()
        return carry

    lax.fori_loop(1, 16, send_z, 0)

    def turns(turn, carry):
        @pl.when(turn < 16)
        def _():
            @pl.when(turn > 0)
            def _():
                along_z(source_offset(turn)).wait_recv()

            for d in (1, 0, 2):
                along_y(turn, d).start()

        @pl.when((turn >= Y_LAG) & (turn < 16 + Y_LAG))
        def _():
            for d in range(3):
                along_y(turn - Y_LAG, d).wait_recv()
            along_x(turn - Y_LAG).start()
            across(turn - Y_LAG, 0).start()

        @pl.when(turn >= Y_LAG + X_LAG)
        def _():
            along_x(turn - Y_LAG - X_LAG).wait_recv()
            across(turn - Y_LAG - X_LAG, 1).start()

        return carry

    lax.fori_loop(0, 16 + Y_LAG + X_LAG, turns, 0)

    def widen(shifts):
        def one_row(row, carry):
            for shift in shifts:
                for half in range(2):
                    source = other if shift % 2 else held
                    index = (shift + 3) // 2 if shift % 2 else (shift + 2) // 2 + core
                    wide = source[index, row, 2 * half : 2 * half + 2].reshape(32, 256).astype(jnp.float32)
                    for lanes in range(2):
                        piece = wide[:, lanes * 128 : lanes * 128 + 128]
                        planes[lanes, shift + 3, 2 * row + half, 0:32] = piece
                        planes[lanes, shift + 3, 2 * row + half, 32:64] = piece
            return carry

        lax.fori_loop(0, 8, one_row, 0)

    widen((-2, 0, 2))

    def drain(turn, carry):
        @pl.when(turn > 0)
        def _():
            along_z(turn).wait_send()

        for d in range(3):
            along_y(turn, d).wait_send()
        along_x(turn).wait_send()
        across(turn, 0).wait()
        across(turn, 1).wait()
        return carry

    lax.fori_loop(0, 16, drain, 0)

    widen((-3, -1, 1, 3))
    fetch.wait()

    def half_sums(odd):
        total[...] = jnp.zeros_like(total)

        def one(entry, carry):
            dx, dy, dz = offsets[0, entry] + 3, offsets[1, entry], offsets[2, entry]
            start = 2 * ((dz + 16) % 16)
            halves = [
                jnp.concatenate(
                    [planes[lanes, dx, (2 * row + odd + dy + 16) % 16, pl.ds(start, 32), :] for row in range(8)], axis=0
                )
                for lanes in range(2)
            ]
            rolled = jnp.concatenate(halves, axis=1).astype(jnp.bfloat16)
            total[...] += jnp.dot(rolled, ops[entry], preferred_element_type=jnp.float32)
            return carry

        lax.fori_loop(0, 16, one, 0)
        part[:, pl.ds(2 * odd, 2)] = total[...].astype(jnp.bfloat16).reshape(8, 2, 16, 256)

    def sum_to(to):
        slot = (to + 3 - y) % 4
        return remote(
            part.at[:, to], from_y.at[slot], sy_send.at[slot], sy_recv.at[slot], device(x, zh, core, zl, to)
        )

    first = 1 - y // 2
    half_sums(first)
    sum_to(2 * first).start()
    sum_to(2 * first + 1).start()
    half_sums(1 - first)
    sum_to(y + 1 - 2 * parity).start()
    sums_y = [sum_to(to) for to in y_of]
    for copy in sums_y:
        copy.wait()
    line = part[:, y].astype(jnp.float32)
    for d in range(3):
        line = line + from_y[d].astype(jnp.float32)
    summed[...] = line
    rounded[...] = line.astype(jnp.bfloat16)
    z_of = [(zl + d) % 8 for d in range(1, 8)]
    sums_z = [
        remote(rounded.at[z_of[d]], from_z.at[d], sz_send.at[d], sz_recv.at[d], device(x, zh, core, z_of[d], y))
        for d in range(7)
    ]
    for copy in sums_z:
        copy.start()
    for copy in sums_z:
        copy.wait()
    result = summed[zl]
    for d in range(7):
        result = result + from_z[d].astype(jnp.float32)
    out[...] = result.reshape(1, 8, 2, 256)


def far_field(fine, upward, offsets, operators):
    dma, half = pltpu.SemaphoreType.DMA, jnp.bfloat16
    return pl.pallas_call(
        far_field_kernel,
        out_shape=jax.ShapeDtypeStruct((1, 8, 2, 256), jnp.float32),
        in_specs=[
            pl.BlockSpec(memory_space=pltpu.VMEM),
            pl.BlockSpec(memory_space=pl.ANY),
            pl.BlockSpec(memory_space=pltpu.SMEM),
            pl.BlockSpec(memory_space=pl.ANY),
        ],
        out_specs=pl.BlockSpec(memory_space=pltpu.VMEM),
        scratch_shapes=[
            pltpu.VMEM((2, 2, 256, 256), half),
            pltpu.VMEM((2, 16, 256), jnp.float32),
            pltpu.VMEM((16, 256), half),
            pltpu.VMEM((16, 256), jnp.float32),
            pltpu.VMEM((4, 8, 4, 16, 256), half),
            pltpu.VMEM((4, 8, 4, 16, 256), half),
            pltpu.VMEM((16, 256, 256), half),
            pltpu.VMEM((2, 7, 16, 64, 128), jnp.float32),
            pltpu.VMEM((256, 256), jnp.float32),
            pltpu.VMEM((8, 4, 16, 256), half),
            pltpu.VMEM((3, 8, 16, 256), half),
            pltpu.VMEM((8, 16, 256), jnp.float32),
            pltpu.VMEM((8, 16, 256), half),
            pltpu.VMEM((7, 16, 256), half),
            dma, dma, dma, dma,
            dma((16,)), dma((16,)),
            dma((16, 3)), dma((16, 3)),
            dma((16,)), dma((16,)),
            dma((16, 2)), dma((16, 2)),
            dma((3,)), dma((3,)), dma((7,)), dma((7,)),
        ],
        compiler_params=pltpu.CompilerParams(collective_id=0, has_side_effects=True),
        name="far_field",
    )(fine, upward, offsets, operators)


def on_device(fine_multipoles, m2m_ops, m2l_ops, offsets):
    return far_field(fine_multipoles, m2m_ops, offsets.T, m2l_ops)


def solution(mesh):
    return jax.shard_map(
        on_device,
        mesh=mesh,
        in_specs=(P("gx", "gy", None, None, None), P(), P("gy", None, None), P("gy", None)),
        out_specs=P("gx", "gy", None, None),
        check_vma=False,
    )
```
